32 devices in a mesh: beam: 2 (over x), chan: 16 (over z, y, core).
Axes of the slice: x: 2, y: 2, z: 4, core: 2. Of those that a mesh axis runs over, the one named last changes fastest.
Arguments:
- spectra: float32 [4096, 1024], P(('beam', 'chan')), parts along dimension 0, may hold values from -6 to 6
- chan_delay: int32 [2048, 32], P('chan'), may hold values from 0 to 63
- window_base: int32 [16, 64], P(None, 'chan'), may hold values from 0 to 28
- trial_offset: int32 [256, 64], P('chan'), may hold values from 0 to 3
- shift_blocks: int32 [256], P('chan'), may hold values from 0 to 7
- template_len: int32 [8], replicated, may hold values from 1 to 128
Outputs:
- scores: float32 [512, 8, 1024], P(('beam', 'chan')), parts along dimension 0
The draws below stay inside these ranges and needn't reach their ends.
There are 2 independent parts, one for each index of `beam`. The reference program is written for one: setup_inputs(seed, part) draws one part's arguments, and reference() takes and returns one part's arrays. A program takes and returns all parts, laid end to end along the dimension named above; an argument that names none is the same for every part. Nothing has to cross between parts.
All inputs are finite; a program needn't handle non-finite values.
Results may differ from the reference program's by a relative error of at most 0.0032.
Values may be sent and summed in bfloat16 or wider, within the bound.
A program may use at most 64 MiB of HBM per device.

```python
import jax
import jax.numpy as jnp
from jax import lax

SUB_CH = 32
NDELAY = 32
MAXD = 64
SPAN = 4
TRIAL_DEV = 16
SAMPLES = 1024
BLOCK = 128
NTEMP = 8
SHIFT_MAX = 7
CHANS = 2048
SUBBANDS = 64
TRIALS = 256
OWNERS = 16


def place_ends(array, rng, smallest, largest):
    extent = array.shape
    place = [jax.random.randint(jax.random.fold_in(rng, axis), (), 0, extent[axis]) for axis in range(len(extent))]
    array = array.at[tuple(place)].set(smallest)
    longest = extent.index(max(extent))
    place[longest] = (place[longest] + 1) % extent[longest]
    return array.at[tuple(place)].set(largest)


def steps_of(own_key, shape, shards, low, top_value):
    loudness, own = 1.0, jax.random.fold_in(own_key, 6)
    for dim, parts in shards:
        heights = jnp.exp(jax.random.uniform(jax.random.fold_in(own, dim), (parts,), jnp.float32, low / len(shards), top_value / len(shards)))
        loudness = loudness * jnp.repeat(heights, shape[dim] // parts).reshape([-1 if axis == dim else 1 for axis in range(len(shape))])
    return loudness


def bell_draw(own_key, shape, scale, reach, cuts=(), kind=jnp.bfloat16):
    gain = steps_of(own_key, shape, cuts, -0.22, 0.18) if cuts else 1.0
    result = jax.random.normal(own_key, shape, jnp.float32) * scale * gain
    return jnp.minimum(jnp.maximum(result, -reach), reach).astype(kind)


def setup_inputs(seed: int = 0, part: int = 0) -> dict:
    key_of = jax.random.split(jax.random.key(seed), 7)
    own_keys = jax.random.split(jax.random.fold_in(key_of[6], part), 7)
    spectra = bell_draw(own_keys[0], (CHANS, SAMPLES), 1.0, 6.0, ((0, 16),), jnp.float32)
    chan_delay = place_ends(jax.random.randint(key_of[1], (CHANS, NDELAY), 0, MAXD), jax.random.fold_in(key_of[1], 1), 0, MAXD - 1).astype(jnp.int32)
    window_base = place_ends(jax.random.randint(key_of[2], (OWNERS, SUBBANDS), 0, NDELAY - SPAN + 1), jax.random.fold_in(key_of[2], 1), 0, NDELAY - SPAN).astype(jnp.int32)
    trial_offset = place_ends(jax.random.randint(key_of[3], (TRIALS, SUBBANDS), 0, SPAN), jax.random.fold_in(key_of[3], 1), 0, SPAN - 1).astype(jnp.int32)
    shift_blocks = place_ends(jax.random.randint(key_of[4], (TRIALS,), 0, SHIFT_MAX + 1), jax.random.fold_in(key_of[4], 1), 0, SHIFT_MAX).astype(jnp.int32)
    template_len = place_ends(jax.random.randint(key_of[5], (NTEMP,), 1, BLOCK + 1), jax.random.fold_in(key_of[5], 1), 1, BLOCK).astype(jnp.int32)
    return {"spectra": spectra, "chan_delay": chan_delay, "window_base": window_base, "trial_offset": trial_offset, "shift_blocks": shift_blocks, "template_len": template_len}


def reference(spectra, chan_delay, window_base, trial_offset, shift_blocks, template_len):
    channels, samples = spectra.shape
    sample_index = jnp.arange(samples, dtype=jnp.int32)

    def one_delay(unused, column):
        source = sample_index[None, :] - column[:, None]
        picked = jnp.take_along_axis(spectra, jnp.clip(source, 0, samples - 1), axis=1)
        picked = jnp.where(source >= 0, picked, jnp.zeros_like(picked))
        summed = picked.reshape(channels // SUB_CH, SUB_CH, samples).sum(axis=1) * SUB_CH ** (-0.5)
        return (unused, summed.astype(jnp.bfloat16))
    _, delay_rows = lax.scan(one_delay, jnp.zeros((), jnp.float32), jnp.transpose(chan_delay))
    trial_delay = (jnp.repeat(window_base, TRIAL_DEV, axis=0) + trial_offset).astype(jnp.int32)

    def add_band(total, band):
        index_col, rows_band = band
        picked = jnp.take(rows_band, index_col, axis=0).astype(jnp.float32)
        return (total + picked, None)
    total, _ = lax.scan(add_band, jnp.zeros((TRIALS, samples), jnp.float32), (jnp.transpose(trial_delay), jnp.transpose(delay_rows, (1, 0, 2))))
    dedispersed = total * SUBBANDS ** (-0.5)
    block_count = samples // BLOCK
    blocks = dedispersed.reshape(TRIALS, block_count, BLOCK)
    source = jnp.arange(block_count, dtype=jnp.int32)[None, :] + shift_blocks[:, None]
    shifted = jnp.take_along_axis(blocks, jnp.clip(source, 0, block_count - 1)[:, :, None], axis=1)
    shifted = jnp.where((source < block_count)[:, :, None], shifted, jnp.zeros_like(shifted))
    flat_shifted = shifted.reshape(TRIALS, samples)
    padded = jnp.pad(flat_shifted, ((0, 0), (1, BLOCK)))
    running = jnp.cumsum(padded, axis=1)
    lower = running[:, :samples]
    outputs = []
    for which_one in range(NTEMP):
        length_now = template_len[which_one]
        upper = lax.dynamic_slice_in_dim(running, length_now.astype(jnp.int32), samples, 1)
        outputs.append((upper - lower) * lax.rsqrt(length_now.astype(jnp.float32)))
    return jnp.stack(outputs, axis=1)
```

```python
import functools

import jax
import jax.numpy as jnp
from jax import lax
from jax.experimental import pallas as pl
from jax.experimental.pallas import tpu as pltpu
from jax.sharding import PartitionSpec as P

SUB_CH = 32
NDELAY = 32
MAXD = 64
SPAN = 4
BLOCK = 128
FINE = 8
COARSE = MAXD // FINE
GROUP = 8
MESH = pl.DeviceIdType.MESH


def split2(value):
    high = value.astype(jnp.bfloat16)
    low = (value - high.astype(jnp.float32)).astype(jnp.bfloat16)
    return high, low


def later(value, steps):
    moved = pltpu.roll(value, steps, 1)
    time = lax.broadcasted_iota(jnp.int32, value.shape, 1)
    return jnp.where(time >= steps, moved, 0.0)


def route_kernel(
    owners, scale_trials, wb_ref, x_hbm, delay_ref, toff_ref, out_ref,
    x, rows, pick, wsend, wown, wrecv, offs, psend, precv,
    x_sem, wsend_sem, wrecv_sem, osend_sem, orecv_sem, psend_sem, precv_sem,
):
    me = lax.axis_index("chan")
    core = lax.rem(me, 2)
    chip = me // 2
    half = owners // 2
    partner = me + 1 - 2 * core
    channels, samples = x.shape
    bands = channels // SUB_CH
    trials, subbands = toff_ref.shape
    wrows = bands * SPAN

    def peer(i):
        return lax.rem(chip + 1 + lax.rem(half // 2 - 1 + i, half - 1), half)

    barrier = pltpu.get_barrier_semaphore()
    loads = []
    for s in range(bands):
        part = pl.ds(s * SUB_CH, SUB_CH)
        load = pltpu.make_async_copy(x_hbm.at[part], x.at[part], x_sem.at[s])
        load.start()
        loads.append(load)
    pl.semaphore_signal(barrier, inc=1, device_id={"chan": partner}, device_id_type=MESH)

    def greet(i, carry):
        pl.semaphore_signal(barrier, inc=1, device_id={"chan": 2 * peer(i) + core}, device_id_type=MESH)
        return carry

    lax.fori_loop(0, half - 1, greet, 0)

    delay = delay_ref[...]
    lane = lax.broadcasted_iota(jnp.int32, delay.shape, 1)
    turned = [delay] + [pltpu.roll(delay, SUB_CH * m, 1) for m in range(1, bands)]

    def one_band(s):
        loads[s].wait()
        spread = turned[(-s) % bands]
        for g in range(1, bands):
            spread = jnp.where(lane // SUB_CH == g, turned[(g - s) % bands], spread)
        spread = spread - lane // SUB_CH
        table = jnp.concatenate(
            [
                jnp.concatenate(
                    [
                        jnp.where(spread == FINE * dh + first, 1.0, 0.0).astype(jnp.bfloat16)
                        for first in range(0, FINE, bands)
                    ],
                    axis=1,
                )
                for dh in range(COARSE)
            ],
            axis=0,
        )
        mine = x[s * SUB_CH : (s + 1) * SUB_CH, :]
        parts = [split2(later(mine, dl) if dl else mine) for dl in range(FINE)]
        high = jnp.concatenate([p[0] for p in parts], axis=0)
        low = jnp.concatenate([p[1] for p in parts], axis=0)
        total = jnp.dot(table, high, preferred_element_type=jnp.float32)
        total = total + jnp.dot(table, low, preferred_element_type=jnp.float32)
        acc = total[(COARSE - 1) * NDELAY :, :]
        for dh in range(COARSE - 2, -1, -1):
            acc = later(acc, FINE) + total[dh * NDELAY : (dh + 1) * NDELAY, :]
        rows[s * NDELAY : (s + 1) * NDELAY, :] = (acc * SUB_CH ** (-0.5)).astype(jnp.bfloat16)

    for s in range(bands // 2):
        one_band(s)

    pl.semaphore_wait(barrier, half)

    def offset_copy(i):
        return pltpu.make_async_remote_copy(
            src_ref=toff_ref, dst_ref=offs.at[chip],
            send_sem=osend_sem.at[peer(i)], recv_sem=orecv_sem.at[chip],
            device_id={"chan": 2 * peer(i) + core}, device_id_type=MESH,
        )

    def send_offset(i, carry):
        offset_copy(i).start()
        return carry

    lax.fori_loop(0, half - 1, send_offset, 0)
    offs[chip] = toff_ref[...]

    for s in range(bands // 2, bands):
        one_band(s)

    wlane = lax.broadcasted_iota(jnp.int32, (wrows, bands * NDELAY), 1)
    wrow = lax.broadcasted_iota(jnp.int32, (wrows, bands * NDELAY), 0)

    def windows(which, target):
        def one_owner(g, carry):
            owner = 2 * g + which
            want = jnp.zeros_like(wrow)
            for s in range(bands):
                want = jnp.where(wrow // SPAN == s, wb_ref[owner, s] + s * NDELAY, want)
            want = want + wrow % SPAN
            start = pl.multiple_of(g * wrows, wrows)
            pick[pl.ds(start, wrows), :] = jnp.where(wlane == want, 1.0, 0.0).astype(jnp.bfloat16)
            return carry

        lax.fori_loop(0, half, one_owner, 0, unroll=min(half, 8))
        for a in range(0, half, GROUP):
            count = min(GROUP, half - a)
            part = jnp.dot(pick[a * wrows : (a + count) * wrows, :], rows[...], preferred_element_type=jnp.float32)
            target[a * wrows : (a + count) * wrows, :] = part.astype(jnp.bfloat16)

    windows(1 - core, wsend)
    pair = pltpu.make_async_remote_copy(
        src_ref=wsend, dst_ref=wrecv, send_sem=wsend_sem, recv_sem=wrecv_sem,
        device_id={"chan": partner}, device_id_type=MESH,
    )
    pair.start()
    windows(core, wown)

    def take_offset(i, carry):
        pltpu.make_async_remote_copy(
            src_ref=toff_ref, dst_ref=offs.at[peer(i)],
            send_sem=osend_sem.at[peer(i)], recv_sem=orecv_sem.at[peer(i)],
            device_id={"chan": 2 * peer(i) + core}, device_id_type=MESH,
        ).wait_recv()
        return carry

    lax.fori_loop(0, half - 1, take_offset, 0)

    groups = [(a, min(GROUP, half - a)) for a in range(0, half, GROUP)]

    def picker(a, count, holder):
        band = lax.broadcasted_iota(jnp.int32, (subbands, count * wrows), 0)
        col = lax.broadcasted_iota(jnp.int32, (subbands, count * wrows), 1)
        expand = jnp.where(band == holder * bands + (col % wrows) // SPAN, 1.0, 0.0).astype(jnp.bfloat16)
        given = offs[a : a + count].reshape(count * trials, subbands)
        given = given.astype(jnp.float32).astype(jnp.bfloat16)
        spread = jnp.dot(given, expand, preferred_element_type=jnp.float32)
        row = lax.broadcasted_iota(jnp.int32, spread.shape, 0)
        col = lax.broadcasted_iota(jnp.int32, spread.shape, 1)
        hit = (row // trials == col // wrows) & (spread == (col % SPAN).astype(jnp.float32))
        return jnp.where(hit, 1.0, 0.0).astype(jnp.bfloat16)

    own_picks = [picker(a, count, me) for a, count in groups]
    far_picks = [picker(a, count, partner) for a, count in groups]
    pair.wait_recv()
    for (a, count), own, far in zip(groups, own_picks, far_picks):
        part = pl.ds(a * wrows, count * wrows)
        total = jnp.dot(own, wown[part, :], preferred_element_type=jnp.float32)
        total = total + jnp.dot(far, wrecv[part, :], preferred_element_type=jnp.float32)
        psend[a : a + count] = total.astype(jnp.bfloat16).reshape(count, trials, samples)

    def partial_copy(i):
        return pltpu.make_async_remote_copy(
            src_ref=psend.at[peer(i)], dst_ref=precv.at[chip],
            send_sem=psend_sem.at[peer(i)], recv_sem=precv_sem.at[chip],
            device_id={"chan": 2 * peer(i) + core}, device_id_type=MESH,
        )

    def send_partial(i, carry):
        partial_copy(i).start()
        return carry

    lax.fori_loop(0, half - 1, send_partial, 0)
    out_ref[...] = psend[chip].astype(jnp.float32)

    def take_partial(i, carry):
        source = peer(half - 2 - i)
        pltpu.make_async_remote_copy(
            src_ref=psend.at[source], dst_ref=precv.at[source],
            send_sem=psend_sem.at[source], recv_sem=precv_sem.at[source],
            device_id={"chan": 2 * source + core}, device_id_type=MESH,
        ).wait_recv()
        out_ref[...] += precv[source].astype(jnp.float32)
        return carry

    lax.fori_loop(0, half - 1, take_partial, 0)
    out_ref[...] = out_ref[...] * scale_trials

    pair.wait_send()

    def finish(i, carry):
        offset_copy(i).wait_send()
        partial_copy(i).wait_send()
        return carry

    lax.fori_loop(0, half - 1, finish, 0)


def score_kernel(shift_ref, length_ref, ded_ref, out_ref):
    trials, samples = ded_ref.shape
    templates = length_ref.shape[0]
    blocks = samples // BLOCK
    ded = ded_ref[...]
    row = lax.broadcasted_iota(jnp.int32, (trials, BLOCK), 0)
    shift = jnp.zeros((trials, BLOCK), jnp.int32)
    for j in range(trials):
        shift = jnp.where(row == j, shift_ref[j], shift)
    zero = jnp.zeros((trials, BLOCK), jnp.float32)
    cols = [ded[:, b * BLOCK : (b + 1) * BLOCK] for b in range(blocks)]
    moved = []
    for b in range(blocks):
        now = zero
        for s in range(blocks - b):
            now = jnp.where(shift == s, cols[b + s], now)
        moved.append(now)
    moved.append(zero)
    here = jnp.concatenate(moved[:-1], axis=0)
    after = jnp.concatenate(moved[1:], axis=0)
    both = jnp.concatenate([here, after], axis=1)
    high, low = split2(both)
    offset = lax.broadcasted_iota(jnp.int32, (2 * BLOCK, BLOCK), 0) - lax.broadcasted_iota(jnp.int32, (2 * BLOCK, BLOCK), 1)
    for i in range(templates):
        length = length_ref[i]
        table = jnp.where((offset >= 0) & (offset < length), 1.0, 0.0).astype(jnp.bfloat16)
        score = jnp.dot(high, table, preferred_element_type=jnp.float32)
        score = score + jnp.dot(low, table, preferred_element_type=jnp.float32)
        weight = lax.rsqrt(jnp.full((trials, BLOCK), length, jnp.int32).astype(jnp.float32))
        for b in range(blocks):
            out_ref[:, i, b * BLOCK : (b + 1) * BLOCK] = score[b * trials : (b + 1) * trials, :] * weight


def local(owners, spectra, chan_delay, window_base, trial_offset, shift_blocks, template_len):
    channels, samples = spectra.shape
    trials, subbands = trial_offset.shape
    half = owners // 2
    bands = channels // SUB_CH
    wrows = bands * SPAN
    vmem = pl.BlockSpec(memory_space=pltpu.VMEM)
    smem = pl.BlockSpec(memory_space=pltpu.SMEM)
    dma = pltpu.SemaphoreType.DMA
    bf16 = jnp.bfloat16
    ded = pl.pallas_call(
        functools.partial(route_kernel, owners, subbands ** (-0.5)),
        out_shape=jax.ShapeDtypeStruct((trials, samples), jnp.float32),
        in_specs=[smem, pl.BlockSpec(memory_space=pl.ANY), vmem, vmem],
        out_specs=vmem,
        scratch_shapes=[
            pltpu.VMEM((channels, samples), jnp.float32),
            pltpu.VMEM((bands * NDELAY, samples), bf16),
            pltpu.VMEM((half * wrows, bands * NDELAY), bf16),
            pltpu.VMEM((half * wrows, samples), bf16),
            pltpu.VMEM((half * wrows, samples), bf16),
            pltpu.VMEM((half * wrows, samples), bf16),
            pltpu.VMEM((half, trials, subbands), jnp.int32),
            pltpu.VMEM((half, trials, samples), bf16),
            pltpu.VMEM((half, trials, samples), bf16),
            dma((bands,)), dma, dma,
            dma((half,)), dma((half,)), dma((half,)), dma((half,)),
        ],
        compiler_params=pltpu.CompilerParams(collective_id=0, has_side_effects=True),
        name="route",
    )(window_base, spectra, jnp.transpose(chan_delay), trial_offset)
    return pl.pallas_call(
        score_kernel,
        out_shape=jax.ShapeDtypeStruct((trials, template_len.shape[0], samples), jnp.float32),
        in_specs=[smem, smem, vmem],
        out_specs=vmem,
        name="score",
    )(shift_blocks, template_len, ded)


def solution(mesh):
    in_specs = (
        P(("beam", "chan"), None),
        P("chan", None),
        P(None, "chan"),
        P("chan", None),
        P("chan"),
        P(),
    )
    out_specs = P(("beam", "chan"), None, None)
    body = functools.partial(local, mesh.shape["chan"])
    return jax.shard_map(body, mesh=mesh, in_specs=in_specs, out_specs=out_specs, check_vma=False)
```

```python
import functools

import jax
import jax.numpy as jnp
from jax import lax
from jax.experimental import pallas as pl
from jax.experimental.pallas import tpu as pltpu
from jax.sharding import PartitionSpec as P

SUB_CH = 32
NDELAY = 32
MAXD = 64
SPAN = 4
BLOCK = 128
FINE = 8
COARSE = MAXD // FINE
GROUP = 8
MESH = pl.DeviceIdType.MESH


def split2(value):
    high = value.astype(jnp.bfloat16)
    low = (value - high.astype(jnp.float32)).astype(jnp.bfloat16)
    return high, low


def later(value, steps):
    moved = pltpu.roll(value, steps, 1)
    time = lax.broadcasted_iota(jnp.int32, value.shape, 1)
    return jnp.where(time >= steps, moved, 0.0)


def route_kernel(
    owners, scale_trials, wb_ref, x_hbm, delay_ref, toff_ref, out_ref,
    x, rows, pick, wsend, wins, picks, mine, psend, precv,
    x_sem, wsend_sem, wrecv_sem, osend_sem, orecv_sem, psend_sem, precv_sem,
):
    me = lax.axis_index("chan")
    core = lax.rem(me, 2)
    chip = me // 2
    half = owners // 2
    partner = me + 1 - 2 * core
    channels, samples = x.shape
    bands = channels // SUB_CH
    trials, subbands = toff_ref.shape
    wrows = bands * SPAN
    upper = (2 * chip) // half
    edge = chip + upper * (half - 1 - 2 * chip)

    def peer(i):
        k = i + 1
        both = (2 * edge - k + 2 * half) // (2 * half)
        near = ((k + 1) // 2) * (2 * (k % 2) - 1)
        far = (k - edge) * (1 - 2 * upper)
        return chip + both * near + (1 - both) * far

    barrier = pltpu.get_barrier_semaphore()
    loads = []
    for s in range(bands):
        part = pl.ds(s * SUB_CH, SUB_CH)
        load = pltpu.make_async_copy(x_hbm.at[part], x.at[part], x_sem.at[s])
        load.start()
        loads.append(load)
    pl.semaphore_signal(barrier, inc=1, device_id={"chan": partner}, device_id_type=MESH)

    def greet(i, carry):
        pl.semaphore_signal(barrier, inc=1, device_id={"chan": 2 * peer(i) + core}, device_id_type=MESH)
        return carry

    lax.fori_loop(0, half - 1, greet, 0)

    band = lax.broadcasted_iota(jnp.int32, (subbands, subbands * SPAN), 0)
    col = lax.broadcasted_iota(jnp.int32, (subbands, subbands * SPAN), 1)
    expand = jnp.where(band == col // SPAN, 1.0, 0.0).astype(jnp.bfloat16)
    given = toff_ref[...].astype(jnp.float32).astype(jnp.bfloat16)
    spread = jnp.dot(given, expand, preferred_element_type=jnp.float32)
    col = lax.broadcasted_iota(jnp.int32, spread.shape, 1)
    hit = jnp.where(spread == (col % SPAN).astype(jnp.float32), 1.0, 0.0)
    for p in range(half):
        mine[p] = hit[:, 2 * wrows * p : 2 * wrows * (p + 1)].astype(jnp.bfloat16)

    delay = delay_ref[...]
    lane = lax.broadcasted_iota(jnp.int32, delay.shape, 1)
    turned = [delay] + [pltpu.roll(delay, SUB_CH * m, 1) for m in range(1, bands)]

    def one_band(s):
        loads[s].wait()
        spread = turned[(-s) % bands]
        for g in range(1, bands):
            spread = jnp.where(lane // SUB_CH == g, turned[(g - s) % bands], spread)
        spread = spread - lane // SUB_CH
        table = jnp.concatenate(
            [
                jnp.concatenate(
                    [
                        jnp.where(spread == FINE * dh + first, 1.0, 0.0).astype(jnp.bfloat16)
                        for first in range(0, FINE, bands)
                    ],
                    axis=1,
                )
                for dh in range(COARSE)
            ],
            axis=0,
        )
        mine = x[s * SUB_CH : (s + 1) * SUB_CH, :]
        parts = [split2(later(mine, dl) if dl else mine) for dl in range(FINE)]
        high = jnp.concatenate([p[0] for p in parts], axis=0)
        low = jnp.concatenate([p[1] for p in parts], axis=0)
        total = jnp.dot(table, high, preferred_element_type=jnp.float32)
        total = total + jnp.dot(table, low, preferred_element_type=jnp.float32)
        acc = total[(COARSE - 1) * NDELAY :, :]
        for dh in range(COARSE - 2, -1, -1):
            acc = later(acc, FINE) + total[dh * NDELAY : (dh + 1) * NDELAY, :]
        rows[s * NDELAY : (s + 1) * NDELAY, :] = (acc * SUB_CH ** (-0.5)).astype(jnp.bfloat16)

    for s in range(bands // 2):
        one_band(s)

    pl.semaphore_wait(barrier, half)

    def picker_copy(i):
        return pltpu.make_async_remote_copy(
            src_ref=mine.at[peer(i)], dst_ref=picks.at[chip],
            send_sem=osend_sem.at[peer(i)], recv_sem=orecv_sem.at[chip],
            device_id={"chan": 2 * peer(i) + core}, device_id_type=MESH,
        )

    def send_picker(i, carry):
        picker_copy(i).start()
        return carry

    lax.fori_loop(0, half - 1, send_picker, 0)

    for s in range(bands // 2, bands):
        one_band(s)

    wlane = lax.broadcasted_iota(jnp.int32, (wrows, bands * NDELAY), 1)
    wrow = lax.broadcasted_iota(jnp.int32, (wrows, bands * NDELAY), 0)

    def windows(which, put):
        def one_owner(g, carry):
            owner = 2 * g + which
            want = jnp.zeros_like(wrow)
            for s in range(bands):
                want = jnp.where(wrow // SPAN == s, wb_ref[s, owner] + s * NDELAY, want)
            want = want + wrow % SPAN
            start = pl.multiple_of(g * wrows, wrows)
            pick[pl.ds(start, wrows), :] = jnp.where(wlane == want, 1.0, 0.0).astype(jnp.bfloat16)
            return carry

        lax.fori_loop(0, half, one_owner, 0, unroll=min(half, 8))
        for a in range(0, half, GROUP):
            count = min(GROUP, half - a)
            part = jnp.dot(pick[a * wrows : (a + count) * wrows, :], rows[...], preferred_element_type=jnp.float32)
            put(a, count, part.astype(jnp.bfloat16).reshape(count, wrows, samples))

    def put_far(a, count, part):
        wsend[a : a + count] = part

    def put_own(a, count, part):
        wins[a : a + count, pl.ds(pl.multiple_of(core * wrows, wrows), wrows), :] = part

    def pair_copy(g, side):
        return pltpu.make_async_remote_copy(
            src_ref=wsend.at[g], dst_ref=wins.at[g, pl.ds(pl.multiple_of(side * wrows, wrows), wrows)],
            send_sem=wsend_sem.at[g], recv_sem=wrecv_sem.at[g],
            device_id={"chan": partner}, device_id_type=MESH,
        )

    def send_pair(i, carry):
        pair_copy(peer(i), core).start()
        return carry

    windows(1 - core, put_far)
    lax.fori_loop(0, half - 1, send_pair, 0)
    pair_copy(chip, core).start()
    windows(core, put_own)

    def partial_copy(i):
        return pltpu.make_async_remote_copy(
            src_ref=psend.at[peer(i)], dst_ref=precv.at[chip],
            send_sem=psend_sem.at[peer(i)], recv_sem=precv_sem.at[chip],
            device_id={"chan": 2 * peer(i) + core}, device_id_type=MESH,
        )

    def one_partial(i, carry):
        i = half - 2 - i
        g = peer(i)
        pltpu.make_async_remote_copy(
            src_ref=mine.at[g], dst_ref=picks.at[g],
            send_sem=osend_sem.at[g], recv_sem=orecv_sem.at[g],
            device_id={"chan": 2 * g + core}, device_id_type=MESH,
        ).wait_recv()
        pair_copy(g, 1 - core).wait_recv()
        psend[g] = jnp.dot(picks[g], wins[g], preferred_element_type=jnp.float32).astype(jnp.bfloat16)
        partial_copy(i).start()
        return carry

    lax.fori_loop(0, half - 1, one_partial, 0)
    pair_copy(chip, 1 - core).wait_recv()
    out_ref[...] = jnp.dot(mine[chip], wins[chip], preferred_element_type=jnp.float32)

    def take_partial(i, carry):
        source = peer(i)
        pltpu.make_async_remote_copy(
            src_ref=psend.at[source], dst_ref=precv.at[source],
            send_sem=psend_sem.at[source], recv_sem=precv_sem.at[source],
            device_id={"chan": 2 * source + core}, device_id_type=MESH,
        ).wait_recv()
        out_ref[...] += precv[source].astype(jnp.float32)
        return carry

    lax.fori_loop(0, half - 1, take_partial, 0)
    out_ref[...] = out_ref[...] * scale_trials

    pair_copy(chip, core).wait_send()

    def finish(i, carry):
        picker_copy(i).wait_send()
        pair_copy(peer(i), core).wait_send()
        partial_copy(i).wait_send()
        return carry

    lax.fori_loop(0, half - 1, finish, 0)


def score_kernel(shift_ref, length_ref, ded_ref, out_ref):
    trials, samples = ded_ref.shape
    templates = length_ref.shape[0]
    blocks = samples // BLOCK
    ded = ded_ref[...]
    row = lax.broadcasted_iota(jnp.int32, (trials, BLOCK), 0)
    shift = jnp.zeros((trials, BLOCK), jnp.int32)
    for j in range(trials):
        shift = jnp.where(row == j, shift_ref[j], shift)
    zero = jnp.zeros((trials, BLOCK), jnp.float32)
    cols = [ded[:, b * BLOCK : (b + 1) * BLOCK] for b in range(blocks)]
    moved = []
    for b in range(blocks):
        now = zero
        for s in range(blocks - b):
            now = jnp.where(shift == s, cols[b + s], now)
        moved.append(now)
    moved.append(zero)
    here = jnp.concatenate(moved[:-1], axis=0)
    after = jnp.concatenate(moved[1:], axis=0)
    both = jnp.concatenate([here, after], axis=1)
    high, low = split2(both)
    offset = lax.broadcasted_iota(jnp.int32, (2 * BLOCK, BLOCK), 0) - lax.broadcasted_iota(jnp.int32, (2 * BLOCK, BLOCK), 1)
    for i in range(templates):
        length = length_ref[i]
        table = jnp.where((offset >= 0) & (offset < length), 1.0, 0.0).astype(jnp.bfloat16)
        score = jnp.dot(high, table, preferred_element_type=jnp.float32)
        score = score + jnp.dot(low, table, preferred_element_type=jnp.float32)
        weight = lax.rsqrt(jnp.full((trials, BLOCK), length, jnp.int32).astype(jnp.float32))
        for b in range(blocks):
            out_ref[:, i, b * BLOCK : (b + 1) * BLOCK] = score[b * trials : (b + 1) * trials, :] * weight


def local(owners, spectra, chan_delay, window_base, trial_offset, shift_blocks, template_len):
    channels, samples = spectra.shape
    trials, subbands = trial_offset.shape
    half = owners // 2
    bands = channels // SUB_CH
    wrows = bands * SPAN
    vmem = pl.BlockSpec(memory_space=pltpu.VMEM)
    smem = pl.BlockSpec(memory_space=pltpu.SMEM)
    dma = pltpu.SemaphoreType.DMA
    bf16 = jnp.bfloat16
    ded = pl.pallas_call(
        functools.partial(route_kernel, owners, subbands ** (-0.5)),
        out_shape=jax.ShapeDtypeStruct((trials, samples), jnp.float32),
        in_specs=[smem, pl.BlockSpec(memory_space=pl.ANY), vmem, vmem],
        out_specs=vmem,
        scratch_shapes=[
            pltpu.VMEM((channels, samples), jnp.float32),
            pltpu.VMEM((bands * NDELAY, samples), bf16),
            pltpu.VMEM((half * wrows, bands * NDELAY), bf16),
            pltpu.VMEM((half, wrows, samples), bf16),
            pltpu.VMEM((half, 2 * wrows, samples), bf16),
            pltpu.VMEM((half, trials, 2 * wrows), bf16),
            pltpu.VMEM((half, trials, 2 * wrows), bf16),
            pltpu.VMEM((half, trials, samples), bf16),
            pltpu.VMEM((half, trials, samples), bf16),
            dma((bands,)), dma((half,)), dma((half,)),
            dma((half,)), dma((half,)), dma((half,)), dma((half,)),
        ],
        compiler_params=pltpu.CompilerParams(collective_id=0, has_side_effects=True),
        name="route",
    )(jnp.transpose(window_base), spectra, jnp.transpose(chan_delay), trial_offset)
    return pl.pallas_call(
        score_kernel,
        out_shape=jax.ShapeDtypeStruct((trials, template_len.shape[0], samples), jnp.float32),
        in_specs=[smem, smem, vmem],
        out_specs=vmem,
        name="score",
    )(shift_blocks, template_len, ded)


def solution(mesh):
    in_specs = (
        P(("beam", "chan"), None),
        P("chan", None),
        P(None, "chan"),
        P("chan", None),
        P("chan"),
        P(),
    )
    out_specs = P(("beam", "chan"), None, None)
    body = functools.partial(local, mesh.shape["chan"])
    return jax.shard_map(body, mesh=mesh, in_specs=in_specs, out_specs=out_specs, check_vma=False)
```

```python
import functools

import jax
import jax.numpy as jnp
from jax import lax
from jax.experimental import pallas as pl
from jax.experimental.pallas import tpu as pltpu
from jax.sharding import PartitionSpec as P

SUB_CH = 32
NDELAY = 32
MAXD = 64
SPAN = 4
BLOCK = 128
FINE = 8
COARSE = MAXD // FINE
GROUP = 8
PIECES = 2
MESH = pl.DeviceIdType.MESH


def split2(value):
    high = value.astype(jnp.bfloat16)
    low = (value - high.astype(jnp.float32)).astype(jnp.bfloat16)
    return high, low


def later(value, steps):
    moved = pltpu.roll(value, steps, 1)
    lane = lax.broadcasted_iota(jnp.int32, (value.shape[0], BLOCK), 1)
    first = jnp.where(lane >= steps, moved[:, :BLOCK], jnp.zeros((), value.dtype))
    return jnp.concatenate([first, moved[:, BLOCK:]], axis=1)


def route_kernel(
    owners, scale_trials, wb_ref, x_hbm, delay_ref, toff_ref, out_ref,
    x, rows, pick, wsend, wins, picks, mine, psend, precv,
    x_sem, wsend_sem, wrecv_sem, osend_sem, orecv_sem, psend_sem, precv_sem,
):
    me = lax.axis_index("chan")
    core = lax.rem(me, 2)
    chip = me // 2
    half = owners // 2
    partner = me + 1 - 2 * core
    channels, samples = x.shape
    bands = channels // SUB_CH
    trials, subbands = toff_ref.shape
    wrows = bands * SPAN
    upper = (2 * chip) // half
    edge = chip + upper * (half - 1 - 2 * chip)

    def peer(i):
        k = i + 1
        both = (2 * edge - k + 2 * half) // (2 * half)
        near = ((k + 1) // 2) * (2 * (k % 2) - 1)
        far = (k - edge) * (1 - 2 * upper)
        return chip + both * near + (1 - both) * far

    barrier = pltpu.get_barrier_semaphore()
    loads = []
    for s in range(bands):
        part = pl.ds(s * SUB_CH, SUB_CH)
        load = pltpu.make_async_copy(x_hbm.at[part], x.at[part], x_sem.at[s])
        load.start()
        loads.append(load)
    pl.semaphore_signal(barrier, inc=1, device_id={"chan": partner}, device_id_type=MESH)

    def greet(i, carry):
        pl.semaphore_signal(barrier, inc=1, device_id={"chan": 2 * peer(i) + core}, device_id_type=MESH)
        return carry

    lax.fori_loop(0, half - 1, greet, 0)

    band = lax.broadcasted_iota(jnp.int32, (subbands, subbands * SPAN), 0)
    col = lax.broadcasted_iota(jnp.int32, (subbands, subbands * SPAN), 1)
    expand = jnp.where(band == col // SPAN, 1.0, 0.0).astype(jnp.bfloat16)
    given = toff_ref[...].astype(jnp.float32).astype(jnp.bfloat16)
    spread = jnp.dot(given, expand, preferred_element_type=jnp.float32)
    col = lax.broadcasted_iota(jnp.int32, spread.shape, 1)
    hit = jnp.where(spread == (col % SPAN).astype(jnp.float32), 1.0, 0.0)
    for p in range(half):
        mine[p] = hit[:, 2 * wrows * p : 2 * wrows * (p + 1)].astype(jnp.bfloat16)

    delay = delay_ref[...]
    lane = lax.broadcasted_iota(jnp.int32, delay.shape, 1)
    turned = [delay] + [pltpu.roll(delay, SUB_CH * m, 1) for m in range(1, bands)]

    def one_band(s):
        loads[s].wait()
        spread = turned[(-s) % bands]
        for g in range(1, bands):
            spread = jnp.where(lane // SUB_CH == g, turned[(g - s) % bands], spread)
        spread = spread - lane // SUB_CH
        table = jnp.concatenate(
            [
                jnp.concatenate(
                    [
                        jnp.where(spread == FINE * dh + first, 1.0, 0.0).astype(jnp.bfloat16)
                        for first in range(0, FINE, bands)
                    ],
                    axis=1,
                )
                for dh in range(COARSE)
            ],
            axis=0,
        )
        band_x = x[s * SUB_CH : (s + 1) * SUB_CH, :]
        high, low = (
            jnp.concatenate([later(part, dl) if dl else part for dl in range(FINE)], axis=0)
            for part in split2(band_x)
        )
        total = jnp.dot(table, high, preferred_element_type=jnp.float32)
        total = total + jnp.dot(table, low, preferred_element_type=jnp.float32)
        acc = total[(COARSE - 1) * NDELAY :, :]
        for dh in range(COARSE - 2, -1, -1):
            acc = later(acc, FINE) + total[dh * NDELAY : (dh + 1) * NDELAY, :]
        rows[s * NDELAY : (s + 1) * NDELAY, :] = (acc * SUB_CH ** (-0.5)).astype(jnp.bfloat16)

    for s in range(bands // 2):
        one_band(s)

    pl.semaphore_wait(barrier, half)

    def picker_copy(i):
        return pltpu.make_async_remote_copy(
            src_ref=mine.at[peer(i)], dst_ref=picks.at[chip],
            send_sem=osend_sem.at[peer(i)], recv_sem=orecv_sem.at[chip],
            device_id={"chan": 2 * peer(i) + core}, device_id_type=MESH,
        )

    def send_picker(i, carry):
        picker_copy(i).start()
        return carry

    lax.fori_loop(0, half - 1, send_picker, 0)

    for s in range(bands // 2, bands):
        one_band(s)

    wlane = lax.broadcasted_iota(jnp.int32, (wrows, bands * NDELAY), 1)
    wrow = lax.broadcasted_iota(jnp.int32, (wrows, bands * NDELAY), 0)

    def windows(which, put):
        def one_owner(g, carry):
            owner = 2 * g + which
            want = jnp.zeros_like(wrow)
            for s in range(bands):
                want = jnp.where(wrow // SPAN == s, wb_ref[s, owner] + s * NDELAY, want)
            want = want + wrow % SPAN
            start = pl.multiple_of(g * wrows, wrows)
            pick[pl.ds(start, wrows), :] = jnp.where(wlane == want, 1.0, 0.0).astype(jnp.bfloat16)
            return carry

        lax.fori_loop(0, half, one_owner, 0, unroll=min(half, 8))
        for a in range(0, half, GROUP):
            count = min(GROUP, half - a)
            part = jnp.dot(pick[a * wrows : (a + count) * wrows, :], rows[...], preferred_element_type=jnp.float32)
            put(a, count, part.astype(jnp.bfloat16).reshape(count, wrows, samples))

    def put_far(a, count, part):
        wsend[a : a + count] = part

    def put_own(a, count, part):
        wins[a : a + count, pl.ds(pl.multiple_of(core * wrows, wrows), wrows), :] = part

    def pair_copy(g, side):
        return pltpu.make_async_remote_copy(
            src_ref=wsend.at[g], dst_ref=wins.at[g, pl.ds(pl.multiple_of(side * wrows, wrows), wrows)],
            send_sem=wsend_sem.at[g], recv_sem=wrecv_sem.at[g],
            device_id={"chan": partner}, device_id_type=MESH,
        )

    def send_pair(i, carry):
        pair_copy(peer(half - 2 - i), core).start()
        return carry

    windows(1 - core, put_far)
    lax.fori_loop(0, half - 1, send_pair, 0)
    pair_copy(chip, core).start()
    windows(core, put_own)

    def partial_copy(i):
        return pltpu.make_async_remote_copy(
            src_ref=psend.at[peer(i)], dst_ref=precv.at[chip],
            send_sem=psend_sem.at[peer(i)], recv_sem=precv_sem.at[chip],
            device_id={"chan": 2 * peer(i) + core}, device_id_type=MESH,
        )

    def one_partial(i, carry):
        i = half - 2 - i
        g = peer(i)
        pltpu.make_async_remote_copy(
            src_ref=mine.at[g], dst_ref=picks.at[g],
            send_sem=osend_sem.at[g], recv_sem=orecv_sem.at[g],
            device_id={"chan": 2 * g + core}, device_id_type=MESH,
        ).wait_recv()
        pair_copy(g, 1 - core).wait_recv()
        psend[g] = jnp.dot(picks[g], wins[g], preferred_element_type=jnp.float32).astype(jnp.bfloat16)
        partial_copy(i).start()
        return carry

    lax.fori_loop(0, half - 1, one_partial, 0)
    pair_copy(chip, 1 - core).wait_recv()
    out_ref[...] = jnp.dot(mine[chip], wins[chip], preferred_element_type=jnp.float32)

    def take_partial(i, carry):
        source = peer(i)
        pltpu.make_async_remote_copy(
            src_ref=psend.at[source], dst_ref=precv.at[source],
            send_sem=psend_sem.at[source], recv_sem=precv_sem.at[source],
            device_id={"chan": 2 * source + core}, device_id_type=MESH,
        ).wait_recv()
        out_ref[...] += precv[source].astype(jnp.float32)
        return carry

    lax.fori_loop(0, half - 1, take_partial, 0)
    out_ref[...] = out_ref[...] * scale_trials

    pair_copy(chip, core).wait_send()

    def finish(i, carry):
        picker_copy(i).wait_send()
        pair_copy(peer(i), core).wait_send()
        partial_copy(i).wait_send()
        return carry

    lax.fori_loop(0, half - 1, finish, 0)


def score_kernel(shift_ref, length_ref, ded_ref, out_hbm, buf, sem):
    trials, samples = ded_ref.shape
    templates = length_ref.shape[0]
    blocks = samples // BLOCK
    ded = ded_ref[...]
    row = lax.broadcasted_iota(jnp.int32, (trials, BLOCK), 0)
    shift = jnp.zeros((trials, BLOCK), jnp.int32)
    for j in range(trials):
        shift = jnp.where(row == j, shift_ref[j], shift)
    zero = jnp.zeros((trials, BLOCK), jnp.float32)
    cols = [ded[:, b * BLOCK : (b + 1) * BLOCK] for b in range(blocks)]
    moved = []
    for b in range(blocks):
        now = zero
        for s in range(blocks - b):
            now = jnp.where(shift == s, cols[b + s], now)
        moved.append(now)
    moved.append(zero)
    moved = [m.astype(jnp.bfloat16) for m in moved]
    offset = lax.broadcasted_iota(jnp.int32, (2 * BLOCK, BLOCK), 0) - lax.broadcasted_iota(jnp.int32, (2 * BLOCK, BLOCK), 1)
    tables, weights = [], []
    for i in range(templates):
        length = length_ref[i]
        tables.append(jnp.where((offset >= 0) & (offset < length), 1.0, 0.0).astype(jnp.bfloat16))
        weights.append(lax.rsqrt(jnp.full((trials, BLOCK), length, jnp.int32).astype(jnp.float32)))
    step = blocks // PIECES
    copies = []
    for piece in range(PIECES):
        first = piece * step
        here = jnp.concatenate(moved[first : first + step], axis=0)
        after = jnp.concatenate(moved[first + 1 : first + step + 1], axis=0)
        both = jnp.concatenate([here, after], axis=1)
        for i in range(0, templates, 2):
            count = min(2, templates - i)
            score = jnp.dot(both, jnp.concatenate(tables[i : i + count], axis=1), preferred_element_type=jnp.float32)
            for b in range(step):
                for k in range(count):
                    part = score[b * trials : (b + 1) * trials, k * BLOCK : (k + 1) * BLOCK]
                    buf[:, i + k, (first + b) * BLOCK : (first + b + 1) * BLOCK] = part * weights[i + k]
        part = pl.ds(first * BLOCK, step * BLOCK)
        copy = pltpu.make_async_copy(buf.at[:, :, part], out_hbm.at[:, :, part], sem.at[piece])
        copy.start()
        copies.append(copy)
    for copy in copies:
        copy.wait()


def local(owners, spectra, chan_delay, window_base, trial_offset, shift_blocks, template_len):
    channels, samples = spectra.shape
    trials, subbands = trial_offset.shape
    half = owners // 2
    bands = channels // SUB_CH
    wrows = bands * SPAN
    vmem = pl.BlockSpec(memory_space=pltpu.VMEM)
    smem = pl.BlockSpec(memory_space=pltpu.SMEM)
    dma = pltpu.SemaphoreType.DMA
    bf16 = jnp.bfloat16
    ded = pl.pallas_call(
        functools.partial(route_kernel, owners, subbands ** (-0.5)),
        out_shape=jax.ShapeDtypeStruct((trials, samples), jnp.float32),
        in_specs=[smem, pl.BlockSpec(memory_space=pl.ANY), vmem, vmem],
        out_specs=vmem,
        scratch_shapes=[
            pltpu.VMEM((channels, samples), jnp.float32),
            pltpu.VMEM((bands * NDELAY, samples), bf16),
            pltpu.VMEM((half * wrows, bands * NDELAY), bf16),
            pltpu.VMEM((half, wrows, samples), bf16),
            pltpu.VMEM((half, 2 * wrows, samples), bf16),
            pltpu.VMEM((half, trials, 2 * wrows), bf16),
            pltpu.VMEM((half, trials, 2 * wrows), bf16),
            pltpu.VMEM((half, trials, samples), bf16),
            pltpu.VMEM((half, trials, samples), bf16),
            dma((bands,)), dma((half,)), dma((half,)),
            dma((half,)), dma((half,)), dma((half,)), dma((half,)),
        ],
        compiler_params=pltpu.CompilerParams(collective_id=0, has_side_effects=True),
        name="route",
    )(jnp.transpose(window_base), spectra, jnp.transpose(chan_delay), trial_offset)
    return pl.pallas_call(
        score_kernel,
        out_shape=jax.ShapeDtypeStruct((trials, template_len.shape[0], samples), jnp.float32),
        in_specs=[smem, smem, vmem],
        out_specs=pl.BlockSpec(memory_space=pl.ANY),
        scratch_shapes=[pltpu.VMEM((trials, template_len.shape[0], samples), jnp.float32), dma((PIECES,))],
        name="score",
    )(shift_blocks, template_len, ded)


def solution(mesh):
    in_specs = (
        P(("beam", "chan"), None),
        P("chan", None),
        P(None, "chan"),
        P("chan", None),
        P("chan"),
        P(),
    )
    out_specs = P(("beam", "chan"), None, None)
    body = functools.partial(local, mesh.shape["chan"])
    return jax.shard_map(body, mesh=mesh, in_specs=in_specs, out_specs=out_specs, check_vma=False)
```

```python
import functools

import jax
import jax.numpy as jnp
from jax import lax
from jax.experimental import pallas as pl
from jax.experimental.pallas import tpu as pltpu
from jax.sharding import PartitionSpec as P

SUB_CH = 32
NDELAY = 32
MAXD = 64
SPAN = 4
BLOCK = 128
FINE = 8
COARSE = MAXD // FINE
GROUP = 8
PIECES = 2
MESH = pl.DeviceIdType.MESH


def split2(value):
    high = value.astype(jnp.bfloat16)
    low = (value - high.astype(jnp.float32)).astype(jnp.bfloat16)
    return high, low


def later(value, steps):
    moved = pltpu.roll(value, steps, 1)
    lane = lax.broadcasted_iota(jnp.int32, (value.shape[0], BLOCK), 1)
    first = jnp.where(lane >= steps, moved[:, :BLOCK], jnp.zeros((), value.dtype))
    return jnp.concatenate([first, moved[:, BLOCK:]], axis=1)


def route_kernel(
    owners, scale_trials, wb_ref, x_hbm, delay_ref, toff_ref, out_ref,
    x, rows, pick, wsend, wins, picks, mine, psend, precv,
    x_sem, wsend_sem, wrecv_sem, osend_sem, orecv_sem, psend_sem, precv_sem,
):
    me = lax.axis_index("chan")
    core = lax.rem(me, 2)
    chip = me // 2
    half = owners // 2
    partner = me + 1 - 2 * core
    channels, samples = x.shape
    bands = channels // SUB_CH
    trials, subbands = toff_ref.shape
    wrows = bands * SPAN
    upper = (2 * chip) // half
    edge = chip + upper * (half - 1 - 2 * chip)

    def peer(i):
        k = i + 1
        both = (2 * edge - k + 2 * half) // (2 * half)
        near = ((k + 1) // 2) * (2 * (k % 2) - 1)
        far = (k - edge) * (1 - 2 * upper)
        return chip + both * near + (1 - both) * far

    barrier = pltpu.get_barrier_semaphore()
    loads = []
    for s in range(bands):
        part = pl.ds(s * SUB_CH, SUB_CH)
        load = pltpu.make_async_copy(x_hbm.at[part], x.at[part], x_sem.at[s])
        load.start()
        loads.append(load)
    pl.semaphore_signal(barrier, inc=1, device_id={"chan": partner}, device_id_type=MESH)

    def greet(i, carry):
        pl.semaphore_signal(barrier, inc=1, device_id={"chan": 2 * peer(i) + core}, device_id_type=MESH)
        return carry

    lax.fori_loop(0, half - 1, greet, 0)

    band = lax.broadcasted_iota(jnp.int32, (subbands, subbands * SPAN), 0)
    col = lax.broadcasted_iota(jnp.int32, (subbands, subbands * SPAN), 1)
    expand = jnp.where(band == col // SPAN, 1.0, 0.0).astype(jnp.bfloat16)
    given = toff_ref[...].astype(jnp.float32).astype(jnp.bfloat16)
    spread = jnp.dot(given, expand, preferred_element_type=jnp.float32)
    col = lax.broadcasted_iota(jnp.int32, spread.shape, 1)
    hit = jnp.where(spread == (col % SPAN).astype(jnp.float32), 1.0, 0.0)
    for p in range(half):
        mine[p] = hit[:, 2 * wrows * p : 2 * wrows * (p + 1)].astype(jnp.bfloat16)

    wlane = lax.broadcasted_iota(jnp.int32, (wrows, bands * NDELAY), 1)
    wrow = lax.broadcasted_iota(jnp.int32, (wrows, bands * NDELAY), 0)

    def one_owner(g, carry):
        for slot, which in enumerate((1 - core, core)):
            want = jnp.zeros_like(wrow)
            for s in range(bands):
                want = jnp.where(wrow // SPAN == s, wb_ref[s, 2 * g + which] + s * NDELAY, want)
            want = want + wrow % SPAN
            start = pl.multiple_of(g * wrows, wrows)
            pick[slot, pl.ds(start, wrows), :] = jnp.where(wlane == want, 1.0, 0.0).astype(jnp.bfloat16)
        return carry

    lax.fori_loop(0, half, one_owner, 0, unroll=min(half, 8))

    delay = delay_ref[...]
    lane = lax.broadcasted_iota(jnp.int32, delay.shape, 1)
    turned = [delay] + [pltpu.roll(delay, SUB_CH * m, 1) for m in range(1, bands)]

    def one_band(s):
        loads[s].wait()
        spread = turned[(-s) % bands]
        for g in range(1, bands):
            spread = jnp.where(lane // SUB_CH == g, turned[(g - s) % bands], spread)
        spread = spread - lane // SUB_CH
        table = jnp.concatenate(
            [
                jnp.concatenate(
                    [
                        jnp.where(spread == FINE * dh + first, 1.0, 0.0).astype(jnp.bfloat16)
                        for first in range(0, FINE, bands)
                    ],
                    axis=1,
                )
                for dh in range(COARSE)
            ],
            axis=0,
        )
        band_x = x[s * SUB_CH : (s + 1) * SUB_CH, :]
        high, low = (
            jnp.concatenate([later(part, dl) if dl else part for dl in range(FINE)], axis=0)
            for part in split2(band_x)
        )
        total = jnp.dot(jnp.concatenate([table, table], axis=1), jnp.concatenate([high, low], axis=0), preferred_element_type=jnp.float32)
        acc = total[(COARSE - 1) * NDELAY :, :]
        for dh in range(COARSE - 2, -1, -1):
            acc = later(acc, FINE) + total[dh * NDELAY : (dh + 1) * NDELAY, :]
        rows[s * NDELAY : (s + 1) * NDELAY, :] = (acc * SUB_CH ** (-0.5)).astype(jnp.bfloat16)

    for s in range(bands // 2):
        one_band(s)

    pl.semaphore_wait(barrier, half)

    def picker_copy(i):
        return pltpu.make_async_remote_copy(
            src_ref=mine.at[peer(i)], dst_ref=picks.at[chip],
            send_sem=osend_sem.at[peer(i)], recv_sem=orecv_sem.at[chip],
            device_id={"chan": 2 * peer(i) + core}, device_id_type=MESH,
        )

    def send_picker(i, carry):
        picker_copy(i).start()
        return carry

    lax.fori_loop(0, half - 1, send_picker, 0)

    for s in range(bands // 2, bands):
        one_band(s)

    def windows(slot, put):
        for a in range(0, half, GROUP):
            count = min(GROUP, half - a)
            table = pick[slot, a * wrows : (a + count) * wrows, :]
            part = jnp.dot(table, rows[...], preferred_element_type=jnp.float32)
            put(a, count, part.astype(jnp.bfloat16).reshape(count, wrows, samples))

    def put_far(a, count, part):
        wsend[a : a + count] = part

    def put_own(a, count, part):
        wins[a : a + count, pl.ds(pl.multiple_of(core * wrows, wrows), wrows), :] = part

    def pair_copy(g, side):
        return pltpu.make_async_remote_copy(
            src_ref=wsend.at[g], dst_ref=wins.at[g, pl.ds(pl.multiple_of(side * wrows, wrows), wrows)],
            send_sem=wsend_sem.at[g], recv_sem=wrecv_sem.at[g],
            device_id={"chan": partner}, device_id_type=MESH,
        )

    def send_pair(i, carry):
        pair_copy(peer(half - 2 - i), core).start()
        return carry

    windows(0, put_far)
    lax.fori_loop(0, half - 1, send_pair, 0)
    pair_copy(chip, core).start()
    windows(1, put_own)

    def partial_copy(i):
        return pltpu.make_async_remote_copy(
            src_ref=psend.at[peer(i)], dst_ref=precv.at[chip],
            send_sem=psend_sem.at[peer(i)], recv_sem=precv_sem.at[chip],
            device_id={"chan": 2 * peer(i) + core}, device_id_type=MESH,
        )

    def one_partial(i, carry):
        i = half - 2 - i
        g = peer(i)
        pltpu.make_async_remote_copy(
            src_ref=mine.at[g], dst_ref=picks.at[g],
            send_sem=osend_sem.at[g], recv_sem=orecv_sem.at[g],
            device_id={"chan": 2 * g + core}, device_id_type=MESH,
        ).wait_recv()
        pair_copy(g, 1 - core).wait_recv()
        psend[g] = jnp.dot(picks[g], wins[g], preferred_element_type=jnp.float32).astype(jnp.bfloat16)
        partial_copy(i).start()
        return carry

    lax.fori_loop(0, half - 1, one_partial, 0)
    pair_copy(chip, 1 - core).wait_recv()
    out_ref[...] = jnp.dot(mine[chip], wins[chip], preferred_element_type=jnp.float32)

    def take_partial(i, carry):
        source = peer(i)
        pltpu.make_async_remote_copy(
            src_ref=psend.at[source], dst_ref=precv.at[source],
            send_sem=psend_sem.at[source], recv_sem=precv_sem.at[source],
            device_id={"chan": 2 * source + core}, device_id_type=MESH,
        ).wait_recv()
        out_ref[...] += precv[source].astype(jnp.float32)
        return carry

    lax.fori_loop(0, half - 1, take_partial, 0)
    out_ref[...] = out_ref[...] * scale_trials

    pair_copy(chip, core).wait_send()

    def finish(i, carry):
        picker_copy(i).wait_send()
        pair_copy(peer(i), core).wait_send()
        partial_copy(i).wait_send()
        return carry

    lax.fori_loop(0, half - 1, finish, 0)


def score_kernel(shift_ref, length_ref, ded_ref, out_hbm, buf, sem):
    trials, samples = ded_ref.shape
    templates = length_ref.shape[0]
    blocks = samples // BLOCK
    ded = ded_ref[...]
    row = lax.broadcasted_iota(jnp.int32, (trials, BLOCK), 0)
    shift = jnp.zeros((trials, BLOCK), jnp.int32)
    for j in range(trials):
        shift = jnp.where(row == j, shift_ref[j], shift)
    zero = jnp.zeros((trials, BLOCK), jnp.float32)
    cols = [ded[:, b * BLOCK : (b + 1) * BLOCK] for b in range(blocks)]
    moved = []
    for b in range(blocks):
        now = zero
        for s in range(blocks - b):
            now = jnp.where(shift == s, cols[b + s], now)
        moved.append(now)
    moved.append(zero)
    moved = [m.astype(jnp.bfloat16) for m in moved]
    offset = lax.broadcasted_iota(jnp.int32, (2 * BLOCK, BLOCK), 0) - lax.broadcasted_iota(jnp.int32, (2 * BLOCK, BLOCK), 1)
    tables, weights = [], []
    for i in range(templates):
        length = length_ref[i]
        tables.append(jnp.where((offset >= 0) & (offset < length), 1.0, 0.0).astype(jnp.bfloat16))
        weights.append(lax.rsqrt(jnp.full((trials, BLOCK), length, jnp.int32).astype(jnp.float32)))
    step = blocks // PIECES
    copies = []
    for piece in range(PIECES):
        first = piece * step
        here = jnp.concatenate(moved[first : first + step], axis=0)
        after = jnp.concatenate(moved[first + 1 : first + step + 1], axis=0)
        both = jnp.concatenate([here, after], axis=1)
        for i in range(0, templates, 2):
            count = min(2, templates - i)
            score = jnp.dot(both, jnp.concatenate(tables[i : i + count], axis=1), preferred_element_type=jnp.float32)
            for b in range(step):
                for k in range(count):
                    part = score[b * trials : (b + 1) * trials, k * BLOCK : (k + 1) * BLOCK]
                    buf[:, i + k, (first + b) * BLOCK : (first + b + 1) * BLOCK] = part * weights[i + k]
        part = pl.ds(first * BLOCK, step * BLOCK)
        copy = pltpu.make_async_copy(buf.at[:, :, part], out_hbm.at[:, :, part], sem.at[piece])
        copy.start()
        copies.append(copy)
    for copy in copies:
        copy.wait()


def local(owners, spectra, chan_delay, window_base, trial_offset, shift_blocks, template_len):
    channels, samples = spectra.shape
    trials, subbands = trial_offset.shape
    half = owners // 2
    bands = channels // SUB_CH
    wrows = bands * SPAN
    vmem = pl.BlockSpec(memory_space=pltpu.VMEM)
    smem = pl.BlockSpec(memory_space=pltpu.SMEM)
    dma = pltpu.SemaphoreType.DMA
    bf16 = jnp.bfloat16
    ded = pl.pallas_call(
        functools.partial(route_kernel, owners, subbands ** (-0.5)),
        out_shape=jax.ShapeDtypeStruct((trials, samples), jnp.float32),
        in_specs=[smem, pl.BlockSpec(memory_space=pl.ANY), vmem, vmem],
        out_specs=vmem,
        scratch_shapes=[
            pltpu.VMEM((channels, samples), jnp.float32),
            pltpu.VMEM((bands * NDELAY, samples), bf16),
            pltpu.VMEM((2, half * wrows, bands * NDELAY), bf16),
            pltpu.VMEM((half, wrows, samples), bf16),
            pltpu.VMEM((half, 2 * wrows, samples), bf16),
            pltpu.VMEM((half, trials, 2 * wrows), bf16),
            pltpu.VMEM((half, trials, 2 * wrows), bf16),
            pltpu.VMEM((half, trials, samples), bf16),
            pltpu.VMEM((half, trials, samples), bf16),
            dma((bands,)), dma((half,)), dma((half,)),
            dma((half,)), dma((half,)), dma((half,)), dma((half,)),
        ],
        compiler_params=pltpu.CompilerParams(collective_id=0, has_side_effects=True),
        name="route",
    )(jnp.transpose(window_base), spectra, jnp.transpose(chan_delay), trial_offset)
    return pl.pallas_call(
        score_kernel,
        out_shape=jax.ShapeDtypeStruct((trials, template_len.shape[0], samples), jnp.float32),
        in_specs=[smem, smem, vmem],
        out_specs=pl.BlockSpec(memory_space=pl.ANY),
        scratch_shapes=[pltpu.VMEM((trials, template_len.shape[0], samples), jnp.float32), dma((PIECES,))],
        name="score",
    )(shift_blocks, template_len, ded)


def solution(mesh):
    in_specs = (
        P(("beam", "chan"), None),
        P("chan", None),
        P(None, "chan"),
        P("chan", None),
        P("chan"),
        P(),
    )
    out_specs = P(("beam", "chan"), None, None)
    body = functools.partial(local, mesh.shape["chan"])
    return jax.shard_map(body, mesh=mesh, in_specs=in_specs, out_specs=out_specs, check_vma=False)
```
